256 devices in a mesh: segment: 32 (over y_hi, z, core), dp: 8 (over y_lo, x).
Axes of the slice: x: 4, y: 4 (y_hi: 2, y_lo: 2; y = y_hi * 2 + y_lo), z: 8, core: 2. Of those that a mesh axis runs over, the one named last changes fastest.
Arguments:
- incoming: bfloat16 [32, 4, 32, 16, 16, 128], P('segment', None, 'dp'), may hold values from -6 to 6
- fresh: bfloat16 [3, 4, 32, 16, 16, 128], P(None, None, 'dp'), may hold values from -6 to 6
- weights: bfloat16 [32, 2, 1152, 128], P('segment'), may hold values from -0.1875 to 0.1875
- momentum: float32 [32, 2, 1152, 128], P('segment', None, 'dp'), may hold values from -6 to 6
Outputs:
- outgoing: bfloat16 [32, 4, 32, 16, 16, 128], P('segment', None, 'dp')
- new_momentum: float32 [32, 2, 1152, 128], P('segment', None, 'dp')
The draws below stay inside these ranges and needn't reach their ends.
All inputs are finite; a program needn't handle non-finite values.
Results may differ from the reference program's by a relative error of at most 0.023.
Values may be sent and summed in bfloat16 or wider, within the bound.
No kernel may reach another device: no remote copies, remote signals or barrier semaphores. Data moves between devices by JAX's collectives and lax.ppermute only.
A program may use at most 64 MiB of HBM per device.

```python
import jax
import jax.numpy as jnp
from jax import lax

CH = 128
HGT = 16
WID = 16
TICKS = 4
SEGMENTS = 32
BATCH = 32


def shard_levels(stream_key, extent, pieces, smallest, high):
    gain = 1.0
    for position, shards_of in pieces:
        draws = jax.random.uniform(jax.random.fold_in(jax.random.fold_in(stream_key, 6), position), (shards_of,), jnp.float32, smallest / len(pieces), high / len(pieces))
        gain = gain * jnp.repeat(jnp.exp(draws), extent[position] // shards_of).reshape((-1,) + (1,) * (len(extent) - 1 - position))
    return gain


def bell_draw(stream_key, shape, scale, limit, pieces=(), held_as=jnp.bfloat16):
    values = jax.random.normal(stream_key, shape, jnp.float32) * scale
    if len(pieces) > 0:
        values = shard_levels(stream_key, shape, pieces, -0.22, 0.18) * values
    return jnp.clip(values, min=-limit, max=limit).astype(held_as)


def setup_inputs(seed: int = 0) -> dict:
    streams_of = jax.random.split(jax.random.key(seed), 5)
    return {
        "incoming": bell_draw(streams_of[0], (SEGMENTS, 4, BATCH, HGT, WID, CH), 1.0, 6.0, ((0, 32), (2, 8))),
        "fresh": bell_draw(streams_of[1], (TICKS - 1, 4, BATCH, HGT, WID, CH), 1.0, 6.0, ((2, 8),)),
        "weights": bell_draw(streams_of[2], (SEGMENTS, 2, 9 * CH, CH), (9 * CH) ** -0.5, 0.1875, ((0, 32),)),
        "momentum": bell_draw(streams_of[3], (SEGMENTS, 2, 9 * CH, CH), 1.0, 6.0, ((0, 32), (2, 8)), jnp.float32),
    }


def patches(field):
    hgt, wid = (field.shape[1], field.shape[2])
    padded = jnp.pad(field, ((0, 0), (1, 1), (1, 1), (0, 0)))
    return jnp.concatenate([padded[:, a:a + hgt, b:b + wid, :] for a in range(3) for b in range(3)], axis=-1)

def convolve(field, filters):
    cols = patches(field).reshape(-1, filters.shape[0])
    out = jnp.dot(cols, filters, preferred_element_type=jnp.float32)
    return out.reshape(field.shape[:3] + (filters.shape[1],))

def flipped(filters):
    chans = filters.shape[1]
    four = filters.reshape(3, 3, chans, chans)
    return jnp.transpose(four[::-1, ::-1], (0, 1, 3, 2)).reshape(9 * chans, chans)

def filter_grad(field, slope):
    cols = patches(field).reshape(-1, 9 * field.shape[3])
    flat = slope.reshape(-1, slope.shape[3])
    return lax.dot_general(cols, flat, (((0,), (0,)), ((), ())), preferred_element_type=jnp.float32)

def silu_slope(value):
    sig = jax.nn.sigmoid(value)
    return sig * (1.0 + value * (1.0 - sig))

def block(state, filters):
    y_one, y_two, dy_one, dy_two = (state[0], state[1], state[2], state[3])
    w_f, w_g = (filters[0], filters[1])
    act_g = convolve(y_one, w_g)
    x_two = (y_two.astype(jnp.float32) - jax.nn.silu(act_g)).astype(jnp.bfloat16)
    z_g = (dy_two.astype(jnp.float32) * silu_slope(act_g)).astype(jnp.bfloat16)
    dx_one = (dy_one.astype(jnp.float32) + convolve(z_g, flipped(w_g))).astype(jnp.bfloat16)
    act_f = convolve(x_two, w_f)
    x_one = (y_one.astype(jnp.float32) - jax.nn.silu(act_f)).astype(jnp.bfloat16)
    z_f = (dx_one.astype(jnp.float32) * silu_slope(act_f)).astype(jnp.bfloat16)
    dx_two = (dy_two.astype(jnp.float32) + convolve(z_f, flipped(w_f))).astype(jnp.bfloat16)
    grads = jnp.stack([filter_grad(x_two, z_f), filter_grad(y_one, z_g)])
    return (jnp.stack([x_one, x_two, dx_one, dx_two]), grads)

def reference(incoming, fresh, weights, momentum):
    state = incoming
    total = jnp.zeros(momentum.shape, jnp.float32)
    outs = state
    for tick in range(TICKS):
        outs, grads = lax.map(lambda pair: block(pair[0], pair[1]), (state, weights))
        total = total + grads
        if tick < TICKS - 1:
            state = jnp.concatenate([outs[1:], fresh[tick][None]], axis=0)
    new_momentum = 0.9 * momentum + total / (TICKS * BATCH)
    return (outs, new_momentum)
```

```python
import functools

import jax
import jax.numpy as jnp
from jax import lax
from jax.experimental import pallas as pl
from jax.experimental.pallas import tpu as pltpu
from jax.sharding import PartitionSpec as P

TICKS = 4
TAPS = 3
CHUNKS = ((0, 2), (2, 2))
F32, BF16 = jnp.float32, jnp.bfloat16


def passed_along(value, axis):
    count = lax.axis_size(axis)
    return lax.ppermute(value, axis, [(source, source - 1) for source in range(1, count)])


def tap(w, a, b):
    chans = w.shape[1]
    first = (TAPS * a + b) * chans
    return w[first : first + chans, :]


def sides(value, wid):
    rows = value.shape[0]
    col = lax.broadcasted_iota(jnp.int32, value.shape, 0) % wid
    before = jnp.where(col == 0, 0.0, pltpu.roll(value, 1, 0))
    after = jnp.where(col == wid - 1, 0.0, pltpu.roll(value, rows - 1, 0))
    return before, after


def windows(pad, count, hgt):
    return pad[:, count : count + hgt].reshape(-1, pad.shape[-1])


def conv(pad_ref, w, wid):
    hgt, chans = pad_ref.shape[1] - 2, pad_ref.shape[-1]
    field = pad_ref[...]
    lhs = jnp.concatenate([windows(field, a, hgt) for a in range(TAPS)], axis=1)
    rhs = jnp.concatenate(
        [jnp.concatenate([tap(w, a, b) for b in range(TAPS)], axis=1) for a in range(TAPS)], axis=0
    )
    out = jnp.dot(lhs, rhs, preferred_element_type=F32)
    left, mid, right = (out[:, b * chans : (b + 1) * chans] for b in range(TAPS))
    return sides(left, wid)[0] + mid + sides(right, wid)[1]


def conv_back(pads_ref, w):
    hgt = pads_ref.shape[2] - 2
    lhs = jnp.concatenate(
        [windows(pads_ref[b], a, hgt) for a in range(TAPS) for b in range(TAPS)], axis=1
    )
    rhs = jnp.concatenate(
        [tap(w, TAPS - 1 - a, TAPS - 1 - b) for a in range(TAPS) for b in range(TAPS)], axis=1
    )
    return lax.dot_general(lhs, rhs, (((1,), (1,)), ((), ())), preferred_element_type=F32)


def grad_of(field, pads_ref):
    hgt = pads_ref.shape[2] - 2
    cols = jnp.concatenate(
        [
            windows(pads_ref[TAPS - 1 - b], TAPS - 1 - a, hgt)
            for a in range(TAPS)
            for b in range(TAPS)
        ],
        axis=1,
    )
    return lax.dot_general(field, cols, (((0,), (0,)), ((), ())), preferred_element_type=F32)


def put_field(pad_ref, value):
    frames, tall, wid, chans = pad_ref.shape
    pad_ref[:, 1 : tall - 1] = value.reshape(frames, tall - 2, wid, chans)


def put_slope(pads_ref, slope, wid):
    before, after = sides(slope, wid)
    put_field(pads_ref.at[0], before.astype(BF16))
    put_field(pads_ref.at[1], slope.astype(BF16))
    put_field(pads_ref.at[2], after.astype(BF16))


def clear_edges(pads_ref):
    tall = pads_ref.shape[-3]
    lead = pads_ref.shape[:-3]
    zero = jnp.zeros(lead + (1,) + pads_ref.shape[-2:], BF16)
    at = (slice(None),) * len(lead)
    pads_ref[at + (slice(0, 1),)] = zero
    pads_ref[at + (slice(tall - 1, tall),)] = zero


def slopes(act):
    sig = jax.nn.sigmoid(act)
    return act * sig, sig * (1.0 + act * (1.0 - sig))


def block_kernel(cfg, *refs):
    first, frames, begin, tick, last = cfg
    refs = list(refs)
    st_ref, w_ref = refs[:2]
    del refs[:2]
    fresh_ref = None if tick == 0 else refs.pop(0)
    acc_ref = None if begin else refs.pop(0)
    out_ref, sum_ref, xpad, xpad2, zpads, zpads2 = refs[:6]
    hgt, wid, chans = out_ref.shape[2:]
    if tick:
        fbuf, sem = refs[6:]
        is_last = lax.axis_index("segment") == lax.axis_size("segment") - 1

        @pl.when(is_last)
        def _():
            copy = pltpu.make_async_copy(
                fresh_ref.at[tick - 1, :, pl.ds(first, frames)], fbuf, sem
            )
            copy.start()
            copy.wait()

        def part(i):
            return jnp.where(is_last, fbuf[i], st_ref[i]).reshape(-1, chans)
    else:

        def part(i):
            return st_ref[0, i, first : first + frames].reshape(-1, chans)

    clear_edges(xpad)
    clear_edges(xpad2)
    clear_edges(zpads)
    clear_edges(zpads2)
    w_f, w_g = w_ref[0, 0], w_ref[0, 1]

    y_one = part(0)
    put_field(xpad, y_one)
    act, slope = slopes(conv(xpad, w_g, wid))
    x_two = (part(1).astype(F32) - act).astype(BF16)
    put_field(xpad2, x_two)
    put_slope(zpads, part(3).astype(F32) * slope, wid)
    out_ref[1] = x_two.reshape(frames, hgt, wid, chans)
    dx_one = (part(2).astype(F32) + conv_back(zpads, w_g)).astype(BF16)
    out_ref[2] = dx_one.reshape(frames, hgt, wid, chans)

    act, slope = slopes(conv(xpad2, w_f, wid))
    out_ref[0] = (y_one.astype(F32) - act).astype(BF16).reshape(frames, hgt, wid, chans)
    put_slope(zpads2, dx_one.astype(F32) * slope, wid)
    dx_two = part(3).astype(F32) + conv_back(zpads2, w_f)
    out_ref[3] = dx_two.astype(BF16).reshape(frames, hgt, wid, chans)

    grad_g = grad_of(y_one, zpads)
    grad_f = grad_of(x_two, zpads2)
    if not begin:
        grad_f = grad_f + acc_ref[0]
        grad_g = grad_g + acc_ref[1]
    if not last:
        sum_ref[0] = grad_f
        sum_ref[1] = grad_g
    else:
        for b in range(TAPS * TAPS):
            sum_ref[0, pl.ds(b * chans, chans)] = grad_f[:, b * chans : (b + 1) * chans]
            sum_ref[1, pl.ds(b * chans, chans)] = grad_g[:, b * chans : (b + 1) * chans]


def block(state, weights, fresh, acc, first, frames, tick, last):
    hgt, wid, chans = state.shape[-3:]
    vmem = pl.BlockSpec(memory_space=pltpu.VMEM)
    hbm = pl.BlockSpec(memory_space=pl.ANY)
    rows = weights.shape[2]
    args, specs = [state, weights], [vmem, vmem]
    if tick:
        args.append(fresh)
        specs.append(hbm)
    begin = acc is None
    if not begin:
        args.append(acc)
        specs.append(vmem)
    tall = hgt + 2
    scratch = [
        pltpu.VMEM((frames, tall, wid, chans), BF16),
        pltpu.VMEM((frames, tall, wid, chans), BF16),
        pltpu.VMEM((TAPS, frames, tall, wid, chans), BF16),
        pltpu.VMEM((TAPS, frames, tall, wid, chans), BF16),
    ]
    if tick:
        scratch += [pltpu.VMEM((4, frames, hgt, wid, chans), BF16), pltpu.SemaphoreType.DMA]
    sums = (2, rows, chans) if last else (2, chans, rows)
    cells = frames * hgt * wid
    return pl.pallas_call(
        functools.partial(block_kernel, (first, frames, begin, tick, last)),
        out_shape=(
            jax.ShapeDtypeStruct((4, frames, hgt, wid, chans), BF16),
            jax.ShapeDtypeStruct(sums, F32),
        ),
        in_specs=specs,
        out_specs=(vmem, vmem),
        scratch_shapes=scratch,
        compiler_params=pltpu.CompilerParams(vmem_limit_bytes=32 << 20),
        cost_estimate=pl.CostEstimate(
            flops=12 * cells * rows * chans, bytes_accessed=8 * cells * chans * 2, transcendentals=0
        ),
        name=f"block_{tick}_{first}",
    )(*args)


def shards(incoming, fresh, weights, momentum):
    replicas = lax.axis_size("dp")
    states = [incoming for _ in CHUNKS]
    acc = None
    outs = [None] * len(CHUNKS)
    for tick in range(TICKS):
        for i, (first, frames) in enumerate(CHUNKS):
            last = tick == TICKS - 1 and i == len(CHUNKS) - 1
            outs[i], acc = block(states[i], weights, fresh, acc, first, frames, tick, last)
            if tick < TICKS - 1:
                states[i] = passed_along(outs[i], "segment")
    rows = weights.shape[2] // replicas
    me = lax.axis_index("dp")
    parts = acc.reshape(2, replicas, rows, weights.shape[3])

    def piece(k):
        return lax.dynamic_slice_in_dim(parts, me ^ k, 1, 1)[:, 0]

    total = piece(0)
    for k in range(1, replicas):
        got = lax.ppermute(piece(k).astype(BF16), "dp", [(d, d ^ k) for d in range(replicas)])
        total = total + got.astype(F32)
    new_momentum = 0.9 * momentum[0] + total / (TICKS * incoming.shape[2] * replicas)
    return (jnp.concatenate(outs, axis=1)[None], new_momentum[None])


def solution(mesh):
    return jax.shard_map(
        shards,
        mesh=mesh,
        in_specs=(
            P("segment", None, "dp", None, None, None),
            P(None, None, "dp", None, None, None),
            P("segment", None, None, None),
            P("segment", None, "dp", None),
        ),
        out_specs=(P("segment", None, "dp", None, None, None), P("segment", None, "dp", None)),
        check_vma=False,
    )
```

```python
import functools

import jax
import jax.numpy as jnp
from jax import lax
from jax.experimental import pallas as pl
from jax.experimental.pallas import tpu as pltpu
from jax.sharding import PartitionSpec as P

TICKS = 4
TAPS = 3
CHUNKS = ((0, 2), (2, 2))
GRANT = 16 << 20
F32, BF16 = jnp.float32, jnp.bfloat16


def passed_along(value, tick):
    count, replicas = lax.axis_size("segment"), lax.axis_size("dp")
    half, swap = count // 2, replicas // 2
    crossing = {half} | ({half + 1} if tick < TICKS - 2 else set()) | ({half - 1} if tick == 1 else set())
    pairs = [
        (s * replicas + d, (s - 1) * replicas + (d ^ swap if s in crossing else d))
        for s in range(1, count)
        for d in range(replicas)
    ]
    return lax.ppermute(value, ("segment", "dp"), pairs)


def tap(w, a, b):
    chans = w.shape[1]
    first = (TAPS * a + b) * chans
    return w[first : first + chans, :]


def sides(value, wid):
    rows = value.shape[0]
    col = lax.broadcasted_iota(jnp.int32, value.shape, 0) % wid
    before = jnp.where(col == 0, 0.0, pltpu.roll(value, 1, 0))
    after = jnp.where(col == wid - 1, 0.0, pltpu.roll(value, rows - 1, 0))
    return before, after


def windows(pad, count, hgt):
    return pad[:, count : count + hgt].reshape(-1, pad.shape[-1])


def conv(pad_ref, w, wid):
    hgt, chans = pad_ref.shape[1] - 2, pad_ref.shape[-1]
    field = pad_ref[...]
    lhs = jnp.concatenate([windows(field, a, hgt) for a in range(TAPS)], axis=1)
    rhs = jnp.concatenate(
        [jnp.concatenate([tap(w, a, b) for b in range(TAPS)], axis=1) for a in range(TAPS)], axis=0
    )
    out = jnp.dot(lhs, rhs, preferred_element_type=F32)
    left, mid, right = (out[:, b * chans : (b + 1) * chans] for b in range(TAPS))
    return sides(left, wid)[0] + mid + sides(right, wid)[1]


def conv_back(pads_ref, w):
    hgt = pads_ref.shape[2] - 2
    lhs = jnp.concatenate(
        [windows(pads_ref[b], a, hgt) for a in range(TAPS) for b in range(TAPS)], axis=1
    )
    rhs = jnp.concatenate(
        [tap(w, TAPS - 1 - a, TAPS - 1 - b) for a in range(TAPS) for b in range(TAPS)], axis=1
    )
    return lax.dot_general(lhs, rhs, (((1,), (1,)), ((), ())), preferred_element_type=F32)


def grad_of(field, pads_ref):
    hgt = pads_ref.shape[2] - 2
    cols = jnp.concatenate(
        [
            windows(pads_ref[TAPS - 1 - b], TAPS - 1 - a, hgt)
            for a in range(TAPS)
            for b in range(TAPS)
        ],
        axis=1,
    )
    return lax.dot_general(field, cols, (((0,), (0,)), ((), ())), preferred_element_type=F32)


def put_field(pad_ref, value):
    frames, tall, wid, chans = pad_ref.shape
    pad_ref[:, 1 : tall - 1] = value.reshape(frames, tall - 2, wid, chans)


def put_slope(pads_ref, slope, wid):
    before, after = sides(slope, wid)
    put_field(pads_ref.at[0], before.astype(BF16))
    put_field(pads_ref.at[1], slope.astype(BF16))
    put_field(pads_ref.at[2], after.astype(BF16))


def clear_edges(pads_ref):
    tall = pads_ref.shape[-3]
    lead = pads_ref.shape[:-3]
    zero = jnp.zeros(lead + (1,) + pads_ref.shape[-2:], BF16)
    at = (slice(None),) * len(lead)
    pads_ref[at + (slice(0, 1),)] = zero
    pads_ref[at + (slice(tall - 1, tall),)] = zero


def slopes(act):
    sig = jax.nn.sigmoid(act)
    return act * sig, sig * (1.0 + act * (1.0 - sig))


def fetched(src, dst, sem):
    copy = pltpu.make_async_copy(src, dst, sem)
    copy.start()
    return copy


def frame_kernel(tick, i, *refs):
    first, frames = CHUNKS[i]
    refs = list(refs)
    src_ref, w_ref = refs[:2]
    del refs[:2]
    if tick:
        fresh_ref = refs.pop(0)
    out_ref, kept_ref = refs[:2]
    del refs[:2]
    hgt, wid, chans = out_ref.shape[2:]
    last = tick == TICKS - 1 and i == len(CHUNKS) - 1
    opening = tick == 0 and i == 0
    if opening:
        whole_ref, wout_ref, xpad, xpad2, zpads, zpads2, sems = refs
        at = pl.ds(first, frames)
        near = [
            fetched(src_ref.at[0, n, at], whole_ref.at[n, at], sems.at[n]) for n in (0, 1, 3, 2)
        ]
        wg = fetched(w_ref.at[0, 1], wout_ref.at[1], sems.at[4])
        wf = fetched(w_ref.at[0, 0], wout_ref.at[0], sems.at[5])
        later = pl.ds(first + frames, src_ref.shape[2] - frames)
        rest = fetched(src_ref.at[0, :, later], whole_ref.at[:, later], sems.at[6])
    else:
        xpad, xpad2, zpads, zpads2 = refs[:4]
    if tick:
        fbuf, sem = refs[4:]
        is_last = lax.axis_index("segment") == lax.axis_size("segment") - 1

        @pl.when(is_last)
        def _():
            fetched(fresh_ref.at[tick - 1, :, pl.ds(first, frames)], fbuf, sem).wait()

        def part(n):
            return jnp.where(is_last, fbuf[n], src_ref[n]).reshape(-1, chans)
    else:
        held = whole_ref if opening else src_ref

        def part(n):
            return held[n, first : first + frames].reshape(-1, chans)

    for pad in (xpad, xpad2, zpads, zpads2):
        clear_edges(pad)
    shape = (frames, hgt, wid, chans)
    if opening:
        near[0].wait()
        wg.wait()
        w_ref = wout_ref
    w_g = w_ref[1]
    y_one = part(0)
    kept_ref[0] = y_one
    put_field(xpad, y_one)
    act, slope = slopes(conv(xpad, w_g, wid))
    if opening:
        for copy in near[1:]:
            copy.wait()
    x_two = (part(1).astype(F32) - act).astype(BF16)
    put_field(xpad2, x_two)
    out_ref[1] = x_two.reshape(shape)
    put_slope(zpads, part(3).astype(F32) * slope, wid)
    kept_ref[1] = windows(zpads[1], 1, hgt)
    dx_one = (part(2).astype(F32) + conv_back(zpads, w_g)).astype(BF16)
    out_ref[2] = dx_one.reshape(shape)

    if opening:
        wf.wait()
    w_f = w_ref[0]
    act, slope = slopes(conv(xpad2, w_f, wid))
    out_ref[0] = (y_one.astype(F32) - act).astype(BF16).reshape(shape)
    if last:
        kept_ref[2] = (dx_one.astype(F32) * slope).astype(BF16)
        out_ref[3] = part(3).reshape(shape)
    else:
        put_slope(zpads2, dx_one.astype(F32) * slope, wid)
        kept_ref[2] = windows(zpads2[1], 1, hgt)
        dx_two = part(3).astype(F32) + conv_back(zpads2, w_f)
        out_ref[3] = dx_two.astype(BF16).reshape(shape)
    if opening:
        rest.wait()


VMEM_SPEC = pl.BlockSpec(memory_space=pltpu.VMEM)
HBM_SPEC = pl.BlockSpec(memory_space=pltpu.HBM)


def in_hbm(value):
    return pltpu.with_memory_space_constraint(value, pltpu.HBM)


def pads(frames, tall, wid, chans, lead=()):
    return pltpu.VMEM(lead + (frames, tall, wid, chans), BF16)


def frame_step(tick, i, source, weights, fresh):
    frames = CHUNKS[i][1]
    hgt, wid, chans = source.shape[-3:]
    rows = weights.shape[-2]
    opening = tick == 0 and i == 0
    cells = frames * hgt * wid
    args, specs = [source, weights], [HBM_SPEC if opening else VMEM_SPEC] * 2
    outs = [
        jax.ShapeDtypeStruct((4, frames, hgt, wid, chans), BF16),
        jax.ShapeDtypeStruct((3, cells, chans), BF16),
    ]
    if opening:
        args = [in_hbm(source), in_hbm(weights)]
        outs.append(jax.ShapeDtypeStruct(source.shape[1:], BF16))
        outs.append(jax.ShapeDtypeStruct(weights.shape[1:], BF16))
    if tick:
        args.append(in_hbm(fresh))
        specs.append(HBM_SPEC)
    tall = hgt + 2
    scratch = [pads(frames, tall, wid, chans)] * 2 + [pads(frames, tall, wid, chans, (TAPS,))] * 2
    if opening:
        scratch.append(pltpu.SemaphoreType.DMA((7,)))
    if tick:
        scratch += [pads(frames, hgt, wid, chans, (4,)), pltpu.SemaphoreType.DMA]
    return pl.pallas_call(
        functools.partial(frame_kernel, tick, i),
        out_shape=outs,
        in_specs=specs,
        out_specs=[VMEM_SPEC] * len(outs),
        scratch_shapes=scratch,
        compiler_params=pltpu.CompilerParams(vmem_limit_bytes=GRANT),
        cost_estimate=pl.CostEstimate(
            flops=8 * cells * rows * chans, bytes_accessed=10 * cells * chans * 2, transcendentals=0
        ),
        name=f"frame_{tick}_{i}",
    )(*args)


def grads_kernel(count, begin, last, *refs):
    refs = list(refs)
    outs, kepts = refs[:count], refs[count : 2 * count]
    del refs[: 2 * count]
    acc_ref = None if begin else refs.pop(0)
    zpads = refs.pop()
    full_ref = refs.pop() if last else None
    frames, tall, wid, chans = zpads.shape[2:]
    clear_edges(zpads)
    sums = []
    for branch in range(2):
        fields = []
        begun = 0
        for out_ref, kept_ref in zip(outs, kepts):
            some = out_ref.shape[1]
            slope = kept_ref[2 - branch].astype(F32)
            put_slope_at = zpads.at[branch, :, pl.ds(begun, some)]
            put_slope(put_slope_at, slope, wid)
            fields.append(kept_ref[0] if branch else out_ref[1].reshape(-1, chans))
            begun += some
        field = fields[0] if count == 1 else jnp.concatenate(fields, axis=0)
        total = grad_of(field, zpads.at[branch])
        if not begin:
            total = total + acc_ref[branch]
        sums.append(total)
    if not last:
        refs[0][0] = sums[0]
        refs[0][1] = sums[1]
        return
    for b in range(TAPS * TAPS):
        for branch in range(2):
            full_ref[branch, pl.ds(b * chans, chans)] = sums[branch][:, b * chans : (b + 1) * chans]
    me = lax.axis_index("dp")
    rows = refs[0].shape[1]
    for k, ref in enumerate(refs):
        begins = pl.multiple_of((me ^ k) * rows, 16)
        ref[...] = full_ref[:, pl.ds(begins, rows)].astype(ref.dtype)


def grads_step(outs, kepts, acc, rows, last, name):
    frames, hgt, wid, chans = outs[0].shape[1:]
    frames = sum(out.shape[1] for out in outs)
    begin = acc is None
    args = [*outs, *kepts] + ([] if begin else [acc])
    scratch = [pads(frames, hgt + 2, wid, chans, (2, TAPS))]
    if last:
        replicas = lax.axis_size("dp")
        part = (2, rows // replicas, chans)
        shapes = [jax.ShapeDtypeStruct(part, BF16 if k else F32) for k in range(replicas)]
        scratch.insert(0, pltpu.VMEM((2, rows, chans), F32))
    else:
        shapes = [jax.ShapeDtypeStruct((2, chans, rows), F32)]
    cells = frames * hgt * wid
    return pl.pallas_call(
        functools.partial(grads_kernel, len(outs), begin, last),
        out_shape=shapes,
        in_specs=[VMEM_SPEC] * len(args),
        out_specs=[VMEM_SPEC] * len(shapes),
        scratch_shapes=scratch,
        compiler_params=pltpu.CompilerParams(vmem_limit_bytes=GRANT),
        cost_estimate=pl.CostEstimate(
            flops=4 * cells * rows * chans, bytes_accessed=4 * rows * chans * 4, transcendentals=0
        ),
        name=name,
    )(*args)


def finish_kernel(count, *refs):
    outs, kept_ref, w_ref = refs[:count], refs[count], refs[count + 1]
    whole_ref, zpads, sems = refs[count + 2 :]
    copies = [
        fetched(outs[i], whole_ref.at[0, :, pl.ds(*CHUNKS[i])], sems.at[i])
        for i in range(count - 1)
    ]
    end = outs[-1]
    shape, wid, chans = end.shape[1:], end.shape[3], end.shape[4]
    at = pl.ds(*CHUNKS[-1])
    copies.append(fetched(end.at[:3], whole_ref.at[0, :3, at], sems.at[count - 1]))
    clear_edges(zpads)
    put_slope(zpads, kept_ref[2].astype(F32), wid)
    dx_two = end[3].reshape(-1, chans).astype(F32) + conv_back(zpads, w_ref[0])
    zpads[0, :, 1 : shape[1] + 1] = dx_two.astype(BF16).reshape(shape)
    copies.append(
        fetched(zpads.at[0, :, pl.ds(1, shape[1])], whole_ref.at[0, 3, at], sems.at[count])
    )
    for copy in copies:
        copy.wait()


def finish(outs, kept, weights, frames):
    hgt, wid, chans = outs[-1].shape[2:]
    args = [*outs, kept, weights]
    return pl.pallas_call(
        functools.partial(finish_kernel, len(outs)),
        out_shape=jax.ShapeDtypeStruct((1, 4, frames, hgt, wid, chans), BF16),
        in_specs=[VMEM_SPEC] * len(args),
        out_specs=HBM_SPEC,
        scratch_shapes=[
            pads(CHUNKS[-1][1], hgt + 2, wid, chans, (TAPS,)),
            pltpu.SemaphoreType.DMA((len(outs) + 1,)),
        ],
        compiler_params=pltpu.CompilerParams(vmem_limit_bytes=GRANT),
        cost_estimate=pl.CostEstimate(flops=1 << 27, bytes_accessed=1 << 20, transcendentals=0),
        name="finish",
    )(*args)


def momentum_kernel(scale, mom_ref, *refs):
    out_ref = refs[-1]
    total = refs[0][...]
    for ref in refs[1:-1]:
        total = total + ref[...].astype(F32)
    out_ref[0] = 0.9 * mom_ref[0] + total * scale


def shards(incoming, fresh, weights, momentum):
    replicas = lax.axis_size("dp")
    frames = incoming.shape[2]
    rows = weights.shape[2]
    count = len(CHUNKS)
    source, wts = incoming, weights
    states = [None] * count
    acc = None
    for tick in range(TICKS):
        outs, kepts = [], []
        for i in range(count):
            source = states[i] if tick else (whole if i else incoming)
            got = frame_step(tick, i, source, wts, fresh)
            outs.append(got[0])
            kepts.append(got[1])
            if tick == 0 and i == 0:
                whole, wts = got[2:]
            if tick < TICKS - 1:
                states[i] = passed_along(got[0], tick)
        if tick < TICKS - 1:
            (acc,) = grads_step(outs, kepts, acc, rows, False, f"grads_{tick}")
    if count > 1:
        (acc,) = grads_step(outs[:-1], kepts[:-1], acc, rows, False, "grads_late")
    pieces = grads_step(outs[-1:], kepts[-1:], acc, rows, True, "grads_last")
    terms = [pieces[0]] + [
        lax.ppermute(pieces[k], "dp", [(d, d ^ k) for d in range(replicas)])
        for k in range(1, replicas)
    ]
    outgoing = finish(outs, kepts[-1], wts, frames)
    new_momentum = pl.pallas_call(
        functools.partial(momentum_kernel, 1.0 / (TICKS * frames * replicas)),
        out_shape=jax.ShapeDtypeStruct(momentum.shape, F32),
        in_specs=[VMEM_SPEC] * (1 + replicas),
        out_specs=VMEM_SPEC,
        compiler_params=pltpu.CompilerParams(vmem_limit_bytes=GRANT),
        name="momentum",
    )(momentum, *terms)
    return (outgoing, new_momentum)


def solution(mesh):
    return jax.shard_map(
        shards,
        mesh=mesh,
        in_specs=(
            P("segment", None, "dp", None, None, None),
            P(None, None, "dp", None, None, None),
            P("segment", None, None, None),
            P("segment", None, "dp", None),
        ),
        out_specs=(P("segment", None, "dp", None, None, None), P("segment", None, "dp", None)),
        check_vma=False,
    )
```

```python
import functools

import jax
import jax.numpy as jnp
from jax import lax
from jax.experimental import pallas as pl
from jax.experimental.pallas import tpu as pltpu
from jax.sharding import PartitionSpec as P


TICKS = 4
TAPS = 3
CHUNKS = ((0, 2), (2, 2))
GRANT = 16 << 20
ORDER = (6, 5, 7, 4, 2, 3, 1)
F32, BF16 = jnp.float32, jnp.bfloat16


def passed_along(value, slot):
    count, replicas = lax.axis_size("segment"), lax.axis_size("dp")
    half, swap, per = count // 2, replicas // 2, len(CHUNKS)

    def pairs(sections, tick):
        crossing = {half} | ({half + 1} if tick < TICKS - 2 else set())
        crossing |= {half - 1} if tick == 1 else set()
        return [
            (s * replicas + d, (s - 1) * replicas + (d ^ swap if s in crossing else d))
            for s in sections
            for d in range(replicas)
        ]

    sent = per * (TICKS - 1)
    near, over = [], None
    if slot < sent:
        near += pairs(range(half + 1, count), slot // per)
        over = lax.ppermute(value, ("segment", "dp"), pairs([half], slot // per))
    if 0 < slot <= sent:
        near += pairs(range(1, half), (slot - 1) // per)
    return lax.ppermute(value, ("segment", "dp"), near), over


def tap(w, a, b):
    chans = w.shape[1]
    first = (TAPS * a + b) * chans
    return w[first : first + chans, :]


def sides(value, wid):
    half = wid // 2
    pair = value.reshape(-1, 2, half, value.shape[-1])
    low, high = pair[:, 0], pair[:, 1]
    at = lax.broadcasted_iota(jnp.int32, low.shape, 1)
    moved = [pltpu.roll(part, 1, 1) for part in (low, high)]
    before = [jnp.where(at == 0, 0.0, moved[0]), jnp.where(at == 0, moved[0], moved[1])]
    moved = [pltpu.roll(part, half - 1, 1) for part in (low, high)]
    after = [
        jnp.where(at == half - 1, moved[1], moved[0]),
        jnp.where(at == half - 1, 0.0, moved[1]),
    ]
    return tuple(jnp.stack(parts, axis=1).reshape(value.shape) for parts in (before, after))


def windows(pad, count, hgt):
    return pad[:, count : count + hgt].reshape(-1, pad.shape[-1])


def conv(pad_ref, w, wid):
    hgt, chans = pad_ref.shape[1] - 2, pad_ref.shape[-1]
    field = pad_ref[...]
    lhs = jnp.concatenate([windows(field, a, hgt) for a in range(TAPS)], axis=1)
    rhs = jnp.concatenate(
        [jnp.concatenate([tap(w, a, b) for b in range(TAPS)], axis=1) for a in range(TAPS)], axis=0
    )
    out = jnp.dot(lhs, rhs, preferred_element_type=F32)
    left, mid, right = (out[:, b * chans : (b + 1) * chans] for b in range(TAPS))
    return sides(left, wid)[0] + mid + sides(right, wid)[1]


def conv_back(pads_ref, w):
    hgt = pads_ref.shape[2] - 2
    lhs = jnp.concatenate(
        [windows(pads_ref[b], a, hgt) for a in range(TAPS) for b in range(TAPS)], axis=1
    )
    rhs = jnp.concatenate(
        [tap(w, TAPS - 1 - a, TAPS - 1 - b) for a in range(TAPS) for b in range(TAPS)], axis=1
    )
    return lax.dot_general(lhs, rhs, (((1,), (1,)), ((), ())), preferred_element_type=F32)


def grad_of(field, pads_ref):
    hgt = pads_ref.shape[2] - 2
    cols = jnp.concatenate(
        [
            windows(pads_ref[TAPS - 1 - b], TAPS - 1 - a, hgt)
            for a in range(TAPS)
            for b in range(TAPS)
        ],
        axis=1,
    )
    return lax.dot_general(field, cols, (((0,), (0,)), ((), ())), preferred_element_type=F32)


def put_field(pad_ref, value):
    frames, tall, wid, chans = pad_ref.shape
    pad_ref[:, 1 : tall - 1] = value.reshape(frames, tall - 2, wid, chans)


def put_slope(pads_ref, slope, wid):
    before, after = sides(slope, wid)
    put_field(pads_ref.at[0], before.astype(BF16))
    put_field(pads_ref.at[1], slope.astype(BF16))
    put_field(pads_ref.at[2], after.astype(BF16))


def clear_edges(pads_ref):
    tall = pads_ref.shape[-3]
    lead = pads_ref.shape[:-3]
    zero = jnp.zeros(lead + (1,) + pads_ref.shape[-2:], BF16)
    at = (slice(None),) * len(lead)
    pads_ref[at + (slice(0, 1),)] = zero
    pads_ref[at + (slice(tall - 1, tall),)] = zero


def slopes(act):
    sig = jax.nn.sigmoid(act)
    out = act * sig
    return out, sig + (out - out * sig)


def fetched(src, dst, sem):
    copy = pltpu.make_async_copy(src, dst, sem)
    copy.start()
    return copy


def places():
    me = lax.axis_index("segment")
    half = lax.axis_size("segment") // 2
    return me < half, me == half - 1, me == lax.axis_size("segment") - 1


def frame_kernel(slot, *refs):
    per, frames = len(CHUNKS), CHUNKS[0][1]
    refs = list(refs)
    opening, last = slot == 0, slot == TICKS * per
    late, joint, newest = places()
    if opening:
        src_ref, w_in = refs[:2]
        out_ref, sum_ref, whole_ref, w_ref, xpad, xpad2, zpads, zpads2, sems = refs[2:]
    else:
        w_ref, acc_ref = refs[:2]
        del refs[:2]
        whole_ref = refs.pop(0) if slot <= per else None
        near_ref = refs.pop(0) if slot >= per else None
        over_ref = refs.pop(0) if slot > per else None
        fresh_ref = refs.pop(0) if per <= slot < TICKS * per else None
        out_ref = refs.pop(0)
        if last:
            kept_ref, full_ref = refs.pop(0), refs.pop()
            pieces = [refs.pop(0) for _ in range(lax.axis_size("dp"))]
        else:
            sum_ref = refs.pop(0)
        xpad, xpad2, zpads, zpads2 = refs[:4]
        if fresh_ref is not None:
            fbuf, sem = refs[4:]

            @pl.when(newest)
            def _():
                at = pl.ds(frames * (slot % per), frames)
                fetched(fresh_ref.at[slot // per - 1, :, at], fbuf, sem).wait()

    hgt, wid, chans = out_ref.shape[2:]
    shape = (frames, hgt, wid, chans)
    if opening:
        at = pl.ds(0, frames)
        first = [
            fetched(src_ref.at[0, n, at], whole_ref.at[n, at], sems.at[n]) for n in (0, 1, 3, 2)
        ]
        wg = fetched(w_in.at[0, 1], w_ref.at[1], sems.at[4])
        wf = fetched(w_in.at[0, 0], w_ref.at[0], sems.at[5])
        later = pl.ds(frames, src_ref.shape[2] - frames)
        rest = fetched(src_ref.at[0, :, later], whole_ref.at[:, later], sems.at[6])

    def part(n):
        if opening:
            value = whole_ref[n, :frames]
        elif slot < per:
            at = pl.multiple_of(frames * (slot - late.astype(jnp.int32)), frames)
            value = whole_ref[n, pl.ds(at, frames)]
        else:
            value = near_ref[n]
            if fresh_ref is not None:
                value = jnp.where(newest, fbuf[n], value)
            if slot == per:
                value = jnp.where(late, whole_ref[n, frames * (per - 1) :], value)
            else:
                value = jnp.where(joint, over_ref[n], value)
        return value.reshape(-1, chans)

    def work():
        for pad in (xpad, xpad2, zpads, zpads2):
            clear_edges(pad)
        if opening:
            first[0].wait()
            wg.wait()
        w_g = w_ref[1]
        y_one = part(0)
        put_field(xpad, y_one)
        act, slope = slopes(conv(xpad, w_g, wid))
        if opening:
            for copy in first[1:]:
                copy.wait()
        x_two = (part(1).astype(F32) - act).astype(BF16)
        put_field(xpad2, x_two)
        out_ref[1] = x_two.reshape(shape)
        put_slope(zpads, part(3).astype(F32) * slope, wid)
        dx_one = (part(2).astype(F32) + conv_back(zpads, w_g)).astype(BF16)
        out_ref[2] = dx_one.reshape(shape)

        if opening:
            wf.wait()
        w_f = w_ref[0]
        act = conv(xpad2, w_f, wid)
        sum_g = grad_of(y_one, zpads)
        if not opening:
            sum_g = sum_g + acc_ref[1]
        if not last:
            sum_ref[1] = sum_g
        act, slope = slopes(act)
        out_ref[0] = (y_one.astype(F32) - act).astype(BF16).reshape(shape)
        put_slope(zpads2, dx_one.astype(F32) * slope, wid)
        sum_f = grad_of(x_two, zpads2)
        if not opening:
            sum_f = sum_f + acc_ref[0]
        if last:
            kept_ref[...] = windows(zpads2[1], 1, hgt)
            out_ref[3] = part(3).reshape(shape)
            spread(full_ref, sum_f, sum_g)
        else:
            sum_ref[0] = sum_f
            dx_two = part(3).astype(F32) + conv_back(zpads2, w_f)
            out_ref[3] = dx_two.astype(BF16).reshape(shape)

    def spread(full_ref, sum_f, sum_g):
        for b in range(TAPS * TAPS):
            at = slice(b * chans, (b + 1) * chans)
            full_ref[0, at] = sum_f[:, at]
            full_ref[1, at] = sum_g[:, at]

    if opening:

        @pl.when(late)
        def _():
            sum_ref[...] = jnp.zeros_like(sum_ref)
            for copy in (*first, wg, wf):
                copy.wait()

        pl.when(jnp.logical_not(late))(work)
        rest.wait()
    elif last:
        pl.when(late)(work)

        @pl.when(jnp.logical_not(late))
        def _():
            spread(full_ref, acc_ref[0], acc_ref[1])

        me = lax.axis_index("dp")
        rows = pieces[0].shape[1]
        for k, ref in enumerate(pieces):
            begins = pl.multiple_of((me ^ k) * rows, 16)
            ref[...] = full_ref[:, pl.ds(begins, rows)].astype(ref.dtype)
    else:
        work()


VMEM_SPEC = pl.BlockSpec(memory_space=pltpu.VMEM)
HBM_SPEC = pl.BlockSpec(memory_space=pltpu.HBM)


def in_hbm(value):
    return pltpu.with_memory_space_constraint(value, pltpu.HBM)


def pads(frames, tall, wid, chans, lead=()):
    return pltpu.VMEM(lead + (frames, tall, wid, chans), BF16)


def frame_step(slot, incoming, fresh, weights, acc, whole, near, over):
    per, frames = len(CHUNKS), CHUNKS[0][1]
    hgt, wid, chans = incoming.shape[-3:]
    rows = weights.shape[-2]
    opening, last = slot == 0, slot == TICKS * per
    cells = frames * hgt * wid
    outs = [jax.ShapeDtypeStruct((4, frames, hgt, wid, chans), BF16)]
    tall = hgt + 2
    scratch = [pads(frames, tall, wid, chans)] * 2 + [pads(frames, tall, wid, chans, (TAPS,))] * 2
    if last:
        replicas = lax.axis_size("dp")
        outs.append(jax.ShapeDtypeStruct((cells, chans), BF16))
        outs += [
            jax.ShapeDtypeStruct((2, rows // replicas, chans), BF16 if k else F32)
            for k in range(replicas)
        ]
    else:
        outs.append(jax.ShapeDtypeStruct((2, chans, rows), F32))
    if opening:
        args = [in_hbm(incoming), in_hbm(weights)]
        specs = [HBM_SPEC] * 2
        outs.append(jax.ShapeDtypeStruct(incoming.shape[1:], BF16))
        outs.append(jax.ShapeDtypeStruct(weights.shape[1:], BF16))
        scratch.append(pltpu.SemaphoreType.DMA((7,)))
    else:
        args = [weights, acc]
        args += [whole] if slot <= per else []
        args += [near] if slot >= per else []
        args += [over] if slot > per else []
        specs = [VMEM_SPEC] * len(args)
        if per <= slot < TICKS * per:
            args.append(in_hbm(fresh))
            specs.append(HBM_SPEC)
            scratch += [pads(frames, hgt, wid, chans, (4,)), pltpu.SemaphoreType.DMA]
        if last:
            scratch.append(pltpu.VMEM((2, rows, chans), F32))
    return pl.pallas_call(
        functools.partial(frame_kernel, slot),
        out_shape=outs,
        in_specs=specs,
        out_specs=[VMEM_SPEC] * len(outs),
        scratch_shapes=scratch,
        compiler_params=pltpu.CompilerParams(vmem_limit_bytes=GRANT),
        cost_estimate=pl.CostEstimate(
            flops=12 * cells * rows * chans, bytes_accessed=10 * cells * chans * 2, transcendentals=0
        ),
    )(*args)


def finish_kernel(early_ref, mid_ref, end_ref, kept_ref, w_ref, whole_ref, zpads, sems):
    late, _, _ = places()
    _, hgt, wid, chans = end_ref.shape[1:]
    firsts = [pl.ds(*chunk) for chunk in CHUNKS]

    @pl.when(jnp.logical_not(late))
    def _():
        one = fetched(early_ref, whole_ref.at[0, :, firsts[0]], sems.at[0])
        two = fetched(mid_ref, whole_ref.at[0, :, firsts[1]], sems.at[1])
        one.wait()
        two.wait()

    @pl.when(late)
    def _():
        one = fetched(mid_ref, whole_ref.at[0, :, firsts[0]], sems.at[0])
        two = fetched(end_ref.at[:3], whole_ref.at[0, :3, firsts[1]], sems.at[1])
        clear_edges(zpads)
        put_slope(zpads, kept_ref[...].astype(F32), wid)
        dx_two = end_ref[3].reshape(-1, chans).astype(F32) + conv_back(zpads, w_ref[0])
        put_field(zpads.at[0], dx_two.astype(BF16))
        three = fetched(
            zpads.at[0, :, pl.ds(1, hgt)], whole_ref.at[0, 3, firsts[1]], sems.at[2]
        )
        one.wait()
        two.wait()
        three.wait()


def finish(early, mid, end, kept, weights, frames):
    hgt, wid, chans = end.shape[2:]
    args = [early, mid, end, kept, weights]
    return pl.pallas_call(
        finish_kernel,
        out_shape=jax.ShapeDtypeStruct((1, 4, frames, hgt, wid, chans), BF16),
        in_specs=[VMEM_SPEC] * len(args),
        out_specs=HBM_SPEC,
        scratch_shapes=[
            pads(end.shape[1], hgt + 2, wid, chans, (TAPS,)),
            pltpu.SemaphoreType.DMA((3,)),
        ],
        compiler_params=pltpu.CompilerParams(vmem_limit_bytes=GRANT),
        cost_estimate=pl.CostEstimate(flops=1 << 27, bytes_accessed=1 << 20, transcendentals=0),
        name="finish",
    )(*args)


def momentum_kernel(scale, mom_ref, *refs):
    out_ref = refs[-1]
    total = refs[0][...]
    for ref in refs[1:-1]:
        total = total + ref[...].astype(F32)
    out_ref[0] = 0.9 * mom_ref[0] + total * scale


def shards(incoming, fresh, weights, momentum):
    replicas = lax.axis_size("dp")
    frames = incoming.shape[2]
    per = len(CHUNKS)
    whole = acc = None
    wts = weights
    outs, nears, overs = [], [], []
    for slot in range(TICKS * per + 1):
        near = nears[slot - per] if slot >= per else None
        over = overs[slot - per - 1] if slot > per else None
        got = frame_step(slot, incoming, fresh, wts, acc, whole, near, over)
        outs.append(got[0])
        acc = got[1]
        if slot == 0:
            whole, wts = got[2:]
        if slot <= per * (TICKS - 1):
            near, over = passed_along(got[0], slot)
            nears.append(near)
            overs.append(over)
    kept, *pieces = got[1:]
    terms = [pieces[0]] + [
        lax.ppermute(pieces[k], "dp", [(d, d ^ k) for d in range(replicas)]) for k in ORDER
    ]
    outgoing = finish(*outs[-3:], kept, wts, frames)
    new_momentum = pl.pallas_call(
        functools.partial(momentum_kernel, 1.0 / (TICKS * frames * replicas)),
        out_shape=jax.ShapeDtypeStruct(momentum.shape, F32),
        in_specs=[VMEM_SPEC] * (1 + replicas),
        out_specs=VMEM_SPEC,
        compiler_params=pltpu.CompilerParams(vmem_limit_bytes=GRANT),
        name="momentum",
    )(momentum, *terms)
    return (outgoing, new_momentum)


def solution(mesh):
    return jax.shard_map(
        shards,
        mesh=mesh,
        in_specs=(
            P("segment", None, "dp", None, None, None),
            P(None, None, "dp", None, None, None),
            P("segment", None, None, None),
            P("segment", None, "dp", None),
        ),
        out_specs=(P("segment", None, "dp", None, None, None), P("segment", None, "dp", None)),
        check_vma=False,
    )
```

```python
import functools

import jax
import jax.numpy as jnp
from jax import lax
from jax.experimental import pallas as pl
from jax.experimental.pallas import tpu as pltpu
from jax.sharding import PartitionSpec as P


TICKS = 4
TAPS = 3
CHUNKS = ((0, 2), (2, 2))
GRANT = 16 << 20
ORDER = (6, 5, 7, 4, 2, 3, 1)
F32, BF16 = jnp.float32, jnp.bfloat16


def passed_along(value, slot):
    count, replicas = lax.axis_size("segment"), lax.axis_size("dp")
    half, swap, per = count // 2, replicas // 2, len(CHUNKS)

    def pairs(sections, tick):
        crossing = {half} | ({half + 1} if tick < TICKS - 2 else set())
        crossing |= {half - 1} if tick == 1 else set()
        return [
            (s * replicas + d, (s - 1) * replicas + (d ^ swap if s in crossing else d))
            for s in sections
            for d in range(replicas)
        ]

    sent = per * (TICKS - 1)
    near, over = [], None
    if slot < sent:
        near += pairs(range(half + 1, count), slot // per)
        over = lax.ppermute(value, ("segment", "dp"), pairs([half], slot // per))
    if 0 < slot <= sent:
        near += pairs(range(1, half), (slot - 1) // per)
    return lax.ppermute(value, ("segment", "dp"), near), over


def tap(w, a, b):
    chans = w.shape[1]
    first = (TAPS * a + b) * chans
    return w[first : first + chans, :]


def sides(value, wid):
    half = wid // 2
    pair = value.reshape(-1, 2, half, value.shape[-1])
    low, high = pair[:, 0], pair[:, 1]
    at = lax.broadcasted_iota(jnp.int32, low.shape, 1)
    moved = [pltpu.roll(part, 1, 1) for part in (low, high)]
    before = [jnp.where(at == 0, 0.0, moved[0]), jnp.where(at == 0, moved[0], moved[1])]
    moved = [pltpu.roll(part, half - 1, 1) for part in (low, high)]
    after = [
        jnp.where(at == half - 1, moved[1], moved[0]),
        jnp.where(at == half - 1, 0.0, moved[1]),
    ]
    return tuple(jnp.stack(parts, axis=1).reshape(value.shape) for parts in (before, after))


def windows(pad, count, hgt):
    return pad[:, count : count + hgt].reshape(-1, pad.shape[-1])


def conv(pad_ref, w, wid):
    hgt, chans = pad_ref.shape[1] - 2, pad_ref.shape[-1]
    field = pad_ref[...]
    lhs = jnp.concatenate([windows(field, a, hgt) for a in range(TAPS)], axis=1)
    rhs = jnp.concatenate(
        [jnp.concatenate([tap(w, a, b) for b in range(TAPS)], axis=1) for a in range(TAPS)], axis=0
    )
    out = jnp.dot(lhs, rhs, preferred_element_type=F32)
    left, mid, right = (out[:, b * chans : (b + 1) * chans] for b in range(TAPS))
    return sides(left, wid)[0] + mid + sides(right, wid)[1]


def conv_back(pads_ref, w):
    hgt = pads_ref.shape[2] - 2
    lhs = jnp.concatenate(
        [windows(pads_ref[b], a, hgt) for a in range(TAPS) for b in range(TAPS)], axis=1
    )
    rhs = jnp.concatenate(
        [tap(w, TAPS - 1 - a, TAPS - 1 - b) for a in range(TAPS) for b in range(TAPS)], axis=1
    )
    return lax.dot_general(lhs, rhs, (((1,), (1,)), ((), ())), preferred_element_type=F32)


def grad_of(field, pads_ref):
    hgt = pads_ref.shape[2] - 2
    cols = jnp.concatenate(
        [
            windows(pads_ref[TAPS - 1 - b], TAPS - 1 - a, hgt)
            for a in range(TAPS)
            for b in range(TAPS)
        ],
        axis=1,
    )
    return lax.dot_general(field, cols, (((0,), (0,)), ((), ())), preferred_element_type=F32)


def put_field(pad_ref, value):
    frames, tall, wid, chans = pad_ref.shape
    pad_ref[:, 1 : tall - 1] = value.reshape(frames, tall - 2, wid, chans)


def put_slope(pads_ref, slope, wid):
    before, after = sides(slope, wid)
    put_field(pads_ref.at[0], before.astype(BF16))
    put_field(pads_ref.at[1], slope.astype(BF16))
    put_field(pads_ref.at[2], after.astype(BF16))


def clear_edges(pads_ref):
    tall = pads_ref.shape[-3]
    lead = pads_ref.shape[:-3]
    zero = jnp.zeros(lead + (1,) + pads_ref.shape[-2:], BF16)
    at = (slice(None),) * len(lead)
    pads_ref[at + (slice(0, 1),)] = zero
    pads_ref[at + (slice(tall - 1, tall),)] = zero


def slopes(act):
    sig = jax.nn.sigmoid(act)
    out = act * sig
    return out, sig + (out - out * sig)


def fetched(src, dst, sem):
    copy = pltpu.make_async_copy(src, dst, sem)
    copy.start()
    return copy


def places():
    me = lax.axis_index("segment")
    half = lax.axis_size("segment") // 2
    return me < half, me == half - 1, me == lax.axis_size("segment") - 1


def frame_kernel(slot, *refs):
    per, frames = len(CHUNKS), CHUNKS[0][1]
    refs = list(refs)
    opening, last = slot == 0, slot == TICKS * per
    late, joint, newest = places()
    if opening:
        src_ref, w_in = refs[:2]
        out_ref, ys_ref, zpads, zpads2, whole_ref, w_ref, xpad, xpad2, sems = refs[2:]
    else:
        w_ref = refs.pop(0)
        acc_ref = refs.pop(0) if last else None
        whole_ref = refs.pop(0) if slot <= per else None
        near_ref = refs.pop(0) if slot >= per else None
        over_ref = refs.pop(0) if slot > per else None
        fresh_ref = refs.pop(0) if per <= slot < TICKS * per else None
        out_ref = refs.pop(0)
        if last:
            kept_ref, full_ref = refs.pop(0), refs.pop()
            pieces = [refs.pop(0) for _ in range(lax.axis_size("dp"))]
            zpads, zpads2 = refs.pop(), refs.pop()
        else:
            ys_ref, zpads, zpads2 = refs[:3]
            del refs[:3]
        xpad, xpad2 = refs[:2]
        if fresh_ref is not None:
            fbuf, sem = refs[2:]

            @pl.when(newest)
            def _():
                at = pl.ds(frames * (slot % per), frames)
                fetched(fresh_ref.at[slot // per - 1, :, at], fbuf, sem).wait()

    hgt, wid, chans = out_ref.shape[2:]
    shape = (hgt, wid, chans)
    if opening:
        at = pl.ds(0, frames)
        first = [
            fetched(src_ref.at[0, n, at], whole_ref.at[n, at], sems.at[n]) for n in (0, 1, 3, 2)
        ]
        wg = fetched(w_in.at[0, 1], w_ref.at[1], sems.at[4])
        wf = fetched(w_in.at[0, 0], w_ref.at[0], sems.at[5])
        later = pl.ds(frames, src_ref.shape[2] - frames)
        rest = fetched(src_ref.at[0, :, later], whole_ref.at[:, later], sems.at[6])

    def part(n, f):
        if opening:
            value = whole_ref[n, f]
        elif slot < per:
            value = whole_ref[n, frames * (slot - late.astype(jnp.int32)) + f]
        else:
            value = near_ref[n, f]
            if fresh_ref is not None:
                value = jnp.where(newest, fbuf[n, f], value)
            if slot == per:
                value = jnp.where(late, whole_ref[n, frames * (per - 1) + f], value)
            else:
                value = jnp.where(joint, over_ref[n, f], value)
        return value.reshape(-1, chans)

    def work():
        each = range(frames)
        for pad in (xpad, xpad2, zpads, zpads2):
            clear_edges(pad)
        if opening:
            first[0].wait()
            wg.wait()
        w_g = w_ref[1]
        y_one = [part(0, f) for f in each]
        for f in each:
            put_field(one(xpad, f), y_one[f])
            if not last:
                ys_ref[pl.ds(f * hgt * wid, hgt * wid)] = y_one[f]
        acts = [conv(one(xpad, f), w_g, wid) for f in each]
        if opening:
            for copy in first[1:]:
                copy.wait()
        x_two = []
        for f in each:
            act, slope = slopes(acts[f])
            x_two.append((part(1, f).astype(F32) - act).astype(BF16))
            put_field(one(xpad2, f), x_two[f])
            out_ref[1, f] = x_two[f].reshape(shape)
            put_slope(zpads.at[:, pl.ds(f, 1)], part(3, f).astype(F32) * slope, wid)
        if opening:
            wf.wait()
        w_f = w_ref[0]
        dx_one, acts = [], []
        for f in each:
            back = conv_back(zpads.at[:, pl.ds(f, 1)], w_g)
            acts.append(conv(one(xpad2, f), w_f, wid))
            dx_one.append((part(2, f).astype(F32) + back).astype(BF16))
            out_ref[2, f] = dx_one[f].reshape(shape)
        if last:
            sum_g = acc_ref[1] + grad_of(jnp.concatenate(y_one, axis=0), zpads)
        for f in each:
            act, slope = slopes(acts[f])
            out_ref[0, f] = (y_one[f].astype(F32) - act).astype(BF16).reshape(shape)
            put_slope(zpads2.at[:, pl.ds(f, 1)], dx_one[f].astype(F32) * slope, wid)
        if not last:
            for f in each:
                dx_two = part(3, f).astype(F32) + conv_back(zpads2.at[:, pl.ds(f, 1)], w_f)
                out_ref[3, f] = dx_two.astype(BF16).reshape(shape)
        if last:
            sum_f = acc_ref[0] + grad_of(jnp.concatenate(x_two, axis=0), zpads2)
            kept_ref[...] = windows(zpads2[1], 1, hgt)
            for f in each:
                out_ref[3, f] = part(3, f).reshape(shape)
            spread(full_ref, sum_f, sum_g)

    def one(pad, f):
        return pad.at[pl.ds(f, 1)]

    def spread(full_ref, sum_f, sum_g):
        for b in range(TAPS * TAPS):
            at = slice(b * chans, (b + 1) * chans)
            full_ref[0, at] = sum_f[:, at]
            full_ref[1, at] = sum_g[:, at]

    if opening:

        @pl.when(late)
        def _():
            for copy in (*first, wg, wf):
                copy.wait()

        pl.when(jnp.logical_not(late))(work)
        rest.wait()
    elif last:
        pl.when(late)(work)

        @pl.when(jnp.logical_not(late))
        def _():
            spread(full_ref, acc_ref[0], acc_ref[1])

        me = lax.axis_index("dp")
        rows = pieces[0].shape[1]
        for k, ref in enumerate(pieces):
            begins = pl.multiple_of((me ^ k) * rows, 16)
            ref[...] = full_ref[:, pl.ds(begins, rows)].astype(ref.dtype)
    else:
        work()


VMEM_SPEC = pl.BlockSpec(memory_space=pltpu.VMEM)
HBM_SPEC = pl.BlockSpec(memory_space=pltpu.HBM)


def in_hbm(value):
    return pltpu.with_memory_space_constraint(value, pltpu.HBM)


def pads(frames, tall, wid, chans, lead=()):
    return pltpu.VMEM(lead + (frames, tall, wid, chans), BF16)


def frame_step(slot, incoming, fresh, weights, acc, whole, near, over):
    per, frames = len(CHUNKS), CHUNKS[0][1]
    hgt, wid, chans = incoming.shape[-3:]
    rows = weights.shape[-2]
    opening, last = slot == 0, slot == TICKS * per
    cells = frames * hgt * wid
    outs = [jax.ShapeDtypeStruct((4, frames, hgt, wid, chans), BF16)]
    tall = hgt + 2
    scratch = [pads(frames, tall, wid, chans)] * 2
    if last:
        replicas = lax.axis_size("dp")
        outs.append(jax.ShapeDtypeStruct((cells, chans), BF16))
        outs += [
            jax.ShapeDtypeStruct((2, rows // replicas, chans), BF16 if k else F32)
            for k in range(replicas)
        ]
    else:
        outs.append(jax.ShapeDtypeStruct((cells, chans), BF16))
        outs += [jax.ShapeDtypeStruct((TAPS, frames, tall, wid, chans), BF16)] * 2
    if opening:
        args = [in_hbm(incoming), in_hbm(weights)]
        specs = [HBM_SPEC] * 2
        outs.append(jax.ShapeDtypeStruct(incoming.shape[1:], BF16))
        outs.append(jax.ShapeDtypeStruct(weights.shape[1:], BF16))
        scratch.append(pltpu.SemaphoreType.DMA((7,)))
    else:
        args = [weights] + ([acc] if last else [])
        args += [whole] if slot <= per else []
        args += [near] if slot >= per else []
        args += [over] if slot > per else []
        specs = [VMEM_SPEC] * len(args)
        if per <= slot < TICKS * per:
            args.append(in_hbm(fresh))
            specs.append(HBM_SPEC)
            scratch += [pads(frames, hgt, wid, chans, (4,)), pltpu.SemaphoreType.DMA]
        if last:
            scratch.append(pltpu.VMEM((2, rows, chans), F32))
            scratch += [pads(frames, tall, wid, chans, (TAPS,))] * 2
            full = scratch.pop(-3)
            scratch.append(full)
    return pl.pallas_call(
        functools.partial(frame_kernel, slot),
        out_shape=outs,
        in_specs=specs,
        out_specs=[VMEM_SPEC] * len(outs),
        scratch_shapes=scratch,
        compiler_params=pltpu.CompilerParams(vmem_limit_bytes=GRANT),
        cost_estimate=pl.CostEstimate(
            flops=8 * cells * rows * chans, bytes_accessed=10 * cells * chans * 2, transcendentals=0
        ),
    )(*args)


def grads_kernel(begin, *refs):
    out_ref, ys_ref, zpads, zpads2 = refs[:4]
    sum_ref = refs[-1]
    late, _, _ = places()

    def work():
        sum_f = grad_of(out_ref[1].reshape(ys_ref.shape), zpads2)
        sum_g = grad_of(ys_ref[...], zpads)
        sum_ref[0] = sum_f if begin else refs[4][0] + sum_f
        sum_ref[1] = sum_g if begin else refs[4][1] + sum_g

    if not begin:
        work()
        return

    @pl.when(late)
    def _():
        sum_ref[...] = jnp.zeros_like(sum_ref)

    pl.when(jnp.logical_not(late))(work)


def grads_step(got, acc, rows):
    begin = acc is None
    cells, chans = got[1].shape
    args = list(got[:4]) + ([] if begin else [acc])
    return pl.pallas_call(
        functools.partial(grads_kernel, begin),
        out_shape=jax.ShapeDtypeStruct((2, chans, rows), F32),
        in_specs=[VMEM_SPEC] * len(args),
        out_specs=VMEM_SPEC,
        compiler_params=pltpu.CompilerParams(vmem_limit_bytes=GRANT),
        cost_estimate=pl.CostEstimate(
            flops=4 * cells * rows * chans, bytes_accessed=4 * rows * chans * 4, transcendentals=0
        ),
    )(*args)


def finish_kernel(early_ref, mid_ref, end_ref, kept_ref, w_ref, whole_ref, zpads, sems):
    late, _, _ = places()
    _, hgt, wid, chans = end_ref.shape[1:]
    firsts = [pl.ds(*chunk) for chunk in CHUNKS]

    @pl.when(jnp.logical_not(late))
    def _():
        one = fetched(early_ref, whole_ref.at[0, :, firsts[0]], sems.at[0])
        two = fetched(mid_ref, whole_ref.at[0, :, firsts[1]], sems.at[1])
        one.wait()
        two.wait()

    @pl.when(late)
    def _():
        one = fetched(mid_ref, whole_ref.at[0, :, firsts[0]], sems.at[0])
        two = fetched(end_ref.at[:3], whole_ref.at[0, :3, firsts[1]], sems.at[1])
        clear_edges(zpads)
        put_slope(zpads, kept_ref[...].astype(F32), wid)
        dx_two = end_ref[3].reshape(-1, chans).astype(F32) + conv_back(zpads, w_ref[0])
        put_field(zpads.at[0], dx_two.astype(BF16))
        three = fetched(
            zpads.at[0, :, pl.ds(1, hgt)], whole_ref.at[0, 3, firsts[1]], sems.at[2]
        )
        one.wait()
        two.wait()
        three.wait()


def finish(early, mid, end, kept, weights, frames):
    hgt, wid, chans = end.shape[2:]
    args = [early, mid, end, kept, weights]
    return pl.pallas_call(
        finish_kernel,
        out_shape=jax.ShapeDtypeStruct((1, 4, frames, hgt, wid, chans), BF16),
        in_specs=[VMEM_SPEC] * len(args),
        out_specs=HBM_SPEC,
        scratch_shapes=[
            pads(end.shape[1], hgt + 2, wid, chans, (TAPS,)),
            pltpu.SemaphoreType.DMA((3,)),
        ],
        compiler_params=pltpu.CompilerParams(vmem_limit_bytes=GRANT),
        cost_estimate=pl.CostEstimate(flops=1 << 27, bytes_accessed=1 << 20, transcendentals=0),
        name="finish",
    )(*args)


def momentum_kernel(scale, mom_ref, *refs):
    out_ref = refs[-1]
    total = refs[0][...]
    for ref in refs[1:-1]:
        total = total + ref[...].astype(F32)
    out_ref[0] = 0.9 * mom_ref[0] + total * scale


def shards(incoming, fresh, weights, momentum):
    replicas = lax.axis_size("dp")
    frames = incoming.shape[2]
    per = len(CHUNKS)
    whole = acc = None
    wts = weights
    outs, nears, overs = [], [], []
    for slot in range(TICKS * per + 1):
        near = nears[slot - per] if slot >= per else None
        over = overs[slot - per - 1] if slot > per else None
        got = frame_step(slot, incoming, fresh, wts, acc, whole, near, over)
        outs.append(got[0])
        if slot == 0:
            whole, wts = got[4:]
        if slot <= per * (TICKS - 1):
            near, over = passed_along(got[0], slot)
            nears.append(near)
            overs.append(over)
        if slot < TICKS * per:
            acc = grads_step(got, acc, weights.shape[2])
    kept, *pieces = got[1:]
    terms = [pieces[0]] + [
        lax.ppermute(pieces[k], "dp", [(d, d ^ k) for d in range(replicas)]) for k in ORDER
    ]
    outgoing = finish(*outs[-3:], kept, wts, frames)
    new_momentum = pl.pallas_call(
        functools.partial(momentum_kernel, 1.0 / (TICKS * frames * replicas)),
        out_shape=jax.ShapeDtypeStruct(momentum.shape, F32),
        in_specs=[VMEM_SPEC] * (1 + replicas),
        out_specs=VMEM_SPEC,
        compiler_params=pltpu.CompilerParams(vmem_limit_bytes=GRANT),
        name="momentum",
    )(momentum, *terms)
    return (outgoing, new_momentum)


def solution(mesh):
    return jax.shard_map(
        shards,
        mesh=mesh,
        in_specs=(
            P("segment", None, "dp", None, None, None),
            P(None, None, "dp", None, None, None),
            P("segment", None, None, None),
            P("segment", None, "dp", None),
        ),
        out_specs=(P("segment", None, "dp", None, None, None), P("segment", None, "dp", None)),
        check_vma=False,
    )
```

```python
import functools

import jax
import jax.numpy as jnp
from jax import lax
from jax.experimental import pallas as pl
from jax.experimental.pallas import tpu as pltpu
from jax.sharding import PartitionSpec as P


TICKS = 4
TAPS = 3
CHUNKS = ((0, 2), (2, 2))
GRANT = 16 << 20
ORDER = (5, 7, 4, 6, 2, 3, 1)
F32, BF16 = jnp.float32, jnp.bfloat16


def passed_along(value, slot):
    count, replicas = lax.axis_size("segment"), lax.axis_size("dp")
    half, swap, per = count // 2, replicas // 2, len(CHUNKS)

    def pairs(sections, tick):
        crossing = {half} | ({half + 1} if tick < TICKS - 2 else set())
        crossing |= {half - 1} if tick == 1 else set()
        return [
            (s * replicas + d, (s - 1) * replicas + (d ^ swap if s in crossing else d))
            for s in sections
            for d in range(replicas)
        ]

    sent = per * (TICKS - 1)
    near, over = [], None
    if slot < sent:
        near += pairs(range(half + 1, count), slot // per)
        over = lax.ppermute(value, ("segment", "dp"), pairs([half], slot // per))
    if 0 < slot <= sent:
        near += pairs(range(1, half), (slot - 1) // per)
    return lax.ppermute(value, ("segment", "dp"), near), over


def tap(w, a, b):
    chans = w.shape[1]
    first = (TAPS * a + b) * chans
    return w[first : first + chans, :]


def sides(value, wid):
    half = wid // 2
    pair = value.reshape(-1, 2, half, value.shape[-1])
    low, high = pair[:, 0], pair[:, 1]
    at = lax.broadcasted_iota(jnp.int32, low.shape, 1)
    moved = [pltpu.roll(part, 1, 1) for part in (low, high)]
    before = [jnp.where(at == 0, 0.0, moved[0]), jnp.where(at == 0, moved[0], moved[1])]
    moved = [pltpu.roll(part, half - 1, 1) for part in (low, high)]
    after = [
        jnp.where(at == half - 1, moved[1], moved[0]),
        jnp.where(at == half - 1, 0.0, moved[1]),
    ]
    return tuple(jnp.stack(parts, axis=1).reshape(value.shape) for parts in (before, after))


def windows(pad, count, hgt):
    return pad[:, count : count + hgt].reshape(-1, pad.shape[-1])


def conv(pad_ref, w, wid):
    hgt, chans = pad_ref.shape[1] - 2, pad_ref.shape[-1]
    field = pad_ref[...]
    lhs = jnp.concatenate([windows(field, a, hgt) for a in range(TAPS)], axis=1)
    rhs = jnp.concatenate(
        [jnp.concatenate([tap(w, a, b) for b in range(TAPS)], axis=1) for a in range(TAPS)], axis=0
    )
    out = jnp.dot(lhs, rhs, preferred_element_type=F32)
    left, mid, right = (out[:, b * chans : (b + 1) * chans] for b in range(TAPS))
    return sides(left, wid)[0] + mid + sides(right, wid)[1]


def conv_back(pad_ref, w):
    _, tall, wid, chans = pad_ref.shape
    field = pad_ref[...]
    lhs = jnp.concatenate([windows(field, a, tall - 2) for a in range(TAPS)], axis=1)
    rhs = jnp.concatenate(
        [
            jnp.concatenate([tap(w, TAPS - 1 - a, TAPS - 1 - b) for a in range(TAPS)], axis=1)
            for b in range(TAPS)
        ],
        axis=0,
    )
    out = lax.dot_general(lhs, rhs, (((1,), (1,)), ((), ())), preferred_element_type=F32)
    left, mid, right = (out[:, b * chans : (b + 1) * chans] for b in range(TAPS))
    return sides(left, wid)[0] + mid + sides(right, wid)[1]


def grad_of(field, pads_ref):
    hgt = pads_ref.shape[2] - 2
    cols = jnp.concatenate(
        [
            windows(pads_ref[TAPS - 1 - b], TAPS - 1 - a, hgt)
            for a in range(TAPS)
            for b in range(TAPS)
        ],
        axis=1,
    )
    return lax.dot_general(field, cols, (((0,), (0,)), ((), ())), preferred_element_type=F32)


def put_field(pad_ref, value):
    frames, tall, wid, chans = pad_ref.shape
    pad_ref[:, 1 : tall - 1] = value.reshape(frames, tall - 2, wid, chans)


def put_slope(pads_ref, slope, wid):
    before, after = sides(slope, wid)
    put_field(pads_ref.at[0], before.astype(BF16))
    put_field(pads_ref.at[1], slope.astype(BF16))
    put_field(pads_ref.at[2], after.astype(BF16))


def put_shifted(pads_ref, pad_ref):
    _, tall, wid, _ = pad_ref.shape
    clear_edges(pads_ref)
    put_slope(pads_ref, windows(pad_ref[...], 1, tall - 2).astype(F32), wid)


def clear_edges(pads_ref):
    tall = pads_ref.shape[-3]
    lead = pads_ref.shape[:-3]
    zero = jnp.zeros(lead + (1,) + pads_ref.shape[-2:], BF16)
    at = (slice(None),) * len(lead)
    pads_ref[at + (slice(0, 1),)] = zero
    pads_ref[at + (slice(tall - 1, tall),)] = zero


def slopes(act):
    sig = jax.nn.sigmoid(act)
    out = act * sig
    return out, sig + (out - out * sig)


def fetched(src, dst, sem):
    copy = pltpu.make_async_copy(src, dst, sem)
    copy.start()
    return copy


def places():
    me = lax.axis_index("segment")
    half = lax.axis_size("segment") // 2
    return me < half, me == half - 1, me == lax.axis_size("segment") - 1


def frame_kernel(slot, *refs):
    per, frames = len(CHUNKS), CHUNKS[0][1]
    refs = list(refs)
    opening, last = slot == 0, slot == TICKS * per
    late, joint, newest = places()
    if opening:
        src_ref, w_in = refs[:2]
        out_ref, ys_ref, zpads, zpads2, whole_ref, w_ref, xpad, xpad2, sems = refs[2:]
    else:
        w_ref = refs.pop(0)
        acc_ref = refs.pop(0) if last else None
        whole_ref = refs.pop(0) if slot <= per else None
        near_ref = refs.pop(0) if slot >= per else None
        over_ref = refs.pop(0) if slot > per else None
        fresh_ref = refs.pop(0) if per <= slot < TICKS * per else None
        out_ref = refs.pop(0)
        if last:
            kept_ref, full_ref = refs.pop(0), refs.pop()
            pieces = [refs.pop(0) for _ in range(lax.axis_size("dp"))]
            zpads, zpads2 = refs.pop(), refs.pop()
            near_g, near_f = refs.pop(), refs.pop()
        else:
            ys_ref, zpads, zpads2 = refs[:3]
            del refs[:3]
        xpad, xpad2 = refs[:2]
        if fresh_ref is not None:
            fbuf, sem = refs[2:]

            @pl.when(newest)
            def _():
                at = pl.ds(frames * (slot % per), frames)
                fetched(fresh_ref.at[slot // per - 1, :, at], fbuf, sem).wait()

    hgt, wid, chans = out_ref.shape[2:]
    shape = (hgt, wid, chans)
    if opening:
        at = pl.ds(0, frames)
        first = [
            fetched(src_ref.at[0, n, at], whole_ref.at[n, at], sems.at[n]) for n in (0, 1, 3, 2)
        ]
        wg = fetched(w_in.at[0, 1], w_ref.at[1], sems.at[4])
        wf = fetched(w_in.at[0, 0], w_ref.at[0], sems.at[5])
        later = pl.ds(frames, src_ref.shape[2] - frames)
        rest = fetched(src_ref.at[0, :, later], whole_ref.at[:, later], sems.at[6])

    def part(n, f):
        if opening:
            value = whole_ref[n, f]
        elif slot < per:
            value = whole_ref[n, frames * (slot - late.astype(jnp.int32)) + f]
        else:
            value = near_ref[n, f]
            if fresh_ref is not None:
                value = jnp.where(newest, fbuf[n, f], value)
            if slot == per:
                value = jnp.where(late, whole_ref[n, frames * (per - 1) + f], value)
            else:
                value = jnp.where(joint, over_ref[n, f], value)
        return value.reshape(-1, chans)

    def work():
        each = range(frames)
        for pad in (xpad, xpad2, zpads, zpads2):
            clear_edges(pad)
        if opening:
            first[0].wait()
            wg.wait()
        w_g = w_ref[1]
        y_one = [part(0, f) for f in each]
        for f in each:
            put_field(one(xpad, f), y_one[f])
            if not last:
                ys_ref[pl.ds(f * hgt * wid, hgt * wid)] = y_one[f]
        acts = [conv(one(xpad, f), w_g, wid) for f in each]
        if opening:
            for copy in first[1:]:
                copy.wait()
        x_two = []
        for f in each:
            act, slope = slopes(acts[f])
            x_two.append((part(1, f).astype(F32) - act).astype(BF16))
            put_field(one(xpad2, f), x_two[f])
            out_ref[1, f] = x_two[f].reshape(shape)
            put_field(one(zpads, f), (part(3, f).astype(F32) * slope).astype(BF16))
        if opening:
            wf.wait()
        w_f = w_ref[0]
        dx_one, acts = [], []
        for f in each:
            back = conv_back(one(zpads, f), w_g)
            acts.append(conv(one(xpad2, f), w_f, wid))
            dx_one.append((part(2, f).astype(F32) + back).astype(BF16))
            out_ref[2, f] = dx_one[f].reshape(shape)
        if last:
            put_shifted(near_g, zpads)
            sum_g = acc_ref[1] + grad_of(jnp.concatenate(y_one, axis=0), near_g)
        for f in each:
            act, slope = slopes(acts[f])
            out_ref[0, f] = (y_one[f].astype(F32) - act).astype(BF16).reshape(shape)
            put_field(one(zpads2, f), (dx_one[f].astype(F32) * slope).astype(BF16))
        if not last:
            for f in each:
                dx_two = part(3, f).astype(F32) + conv_back(one(zpads2, f), w_f)
                out_ref[3, f] = dx_two.astype(BF16).reshape(shape)
        if last:
            put_shifted(near_f, zpads2)
            sum_f = acc_ref[0] + grad_of(jnp.concatenate(x_two, axis=0), near_f)
            kept_ref[...] = windows(zpads2[...], 1, hgt)
            for f in each:
                out_ref[3, f] = part(3, f).reshape(shape)
            spread(full_ref, sum_f, sum_g)

    def one(pad, f):
        return pad.at[pl.ds(f, 1)]

    def spread(full_ref, sum_f, sum_g):
        for b in range(TAPS * TAPS):
            at = slice(b * chans, (b + 1) * chans)
            full_ref[0, at] = sum_f[:, at]
            full_ref[1, at] = sum_g[:, at]

    if opening:

        @pl.when(late)
        def _():
            for copy in (*first, wg, wf):
                copy.wait()

        pl.when(jnp.logical_not(late))(work)
        rest.wait()
    elif last:
        pl.when(late)(work)

        @pl.when(jnp.logical_not(late))
        def _():
            spread(full_ref, acc_ref[0], acc_ref[1])

        me = lax.axis_index("dp")
        rows = pieces[0].shape[1]
        for k, ref in enumerate(pieces):
            begins = pl.multiple_of((me ^ k) * rows, 16)
            ref[...] = full_ref[:, pl.ds(begins, rows)].astype(ref.dtype)
    else:
        work()


VMEM_SPEC = pl.BlockSpec(memory_space=pltpu.VMEM)
HBM_SPEC = pl.BlockSpec(memory_space=pltpu.HBM)


def in_hbm(value):
    return pltpu.with_memory_space_constraint(value, pltpu.HBM)


def pads(frames, tall, wid, chans, lead=()):
    return pltpu.VMEM(lead + (frames, tall, wid, chans), BF16)


def frame_step(slot, incoming, fresh, weights, acc, whole, near, over):
    per, frames = len(CHUNKS), CHUNKS[0][1]
    hgt, wid, chans = incoming.shape[-3:]
    rows = weights.shape[-2]
    opening, last = slot == 0, slot == TICKS * per
    cells = frames * hgt * wid
    outs = [jax.ShapeDtypeStruct((4, frames, hgt, wid, chans), BF16)]
    tall = hgt + 2
    scratch = [pads(frames, tall, wid, chans)] * 2
    if last:
        replicas = lax.axis_size("dp")
        outs.append(jax.ShapeDtypeStruct((cells, chans), BF16))
        outs += [
            jax.ShapeDtypeStruct((2, rows // replicas, chans), BF16 if k else F32)
            for k in range(replicas)
        ]
    else:
        outs.append(jax.ShapeDtypeStruct((cells, chans), BF16))
        outs += [jax.ShapeDtypeStruct((frames, tall, wid, chans), BF16)] * 2
    if opening:
        args = [in_hbm(incoming), in_hbm(weights)]
        specs = [HBM_SPEC] * 2
        outs.append(jax.ShapeDtypeStruct(incoming.shape[1:], BF16))
        outs.append(jax.ShapeDtypeStruct(weights.shape[1:], BF16))
        scratch.append(pltpu.SemaphoreType.DMA((7,)))
    else:
        args = [weights] + ([acc] if last else [])
        args += [whole] if slot <= per else []
        args += [near] if slot >= per else []
        args += [over] if slot > per else []
        specs = [VMEM_SPEC] * len(args)
        if per <= slot < TICKS * per:
            args.append(in_hbm(fresh))
            specs.append(HBM_SPEC)
            scratch += [pads(frames, hgt, wid, chans, (4,)), pltpu.SemaphoreType.DMA]
        if last:
            scratch += [pads(frames, tall, wid, chans, (TAPS,))] * 2
            scratch += [pads(frames, tall, wid, chans)] * 2
            scratch.append(pltpu.VMEM((2, rows, chans), F32))
    return pl.pallas_call(
        functools.partial(frame_kernel, slot),
        out_shape=outs,
        in_specs=specs,
        out_specs=[VMEM_SPEC] * len(outs),
        scratch_shapes=scratch,
        compiler_params=pltpu.CompilerParams(vmem_limit_bytes=GRANT),
        cost_estimate=pl.CostEstimate(
            flops=8 * cells * rows * chans, bytes_accessed=10 * cells * chans * 2, transcendentals=0
        ),
    )(*args)


def grads_kernel(begin, *refs):
    out_ref, ys_ref, zpads, zpads2 = refs[:4]
    sum_ref, near = refs[-2:]
    late, _, _ = places()

    def work():
        put_shifted(near.at[0], zpads2)
        put_shifted(near.at[1], zpads)
        sum_f = grad_of(out_ref[1].reshape(ys_ref.shape), near.at[0])
        sum_g = grad_of(ys_ref[...], near.at[1])
        sum_ref[0] = sum_f if begin else refs[4][0] + sum_f
        sum_ref[1] = sum_g if begin else refs[4][1] + sum_g

    if not begin:
        work()
        return

    @pl.when(late)
    def _():
        sum_ref[...] = jnp.zeros_like(sum_ref)

    pl.when(jnp.logical_not(late))(work)


def grads_step(got, acc, rows):
    begin = acc is None
    cells, chans = got[1].shape
    args = list(got[:4]) + ([] if begin else [acc])
    return pl.pallas_call(
        functools.partial(grads_kernel, begin),
        out_shape=jax.ShapeDtypeStruct((2, chans, rows), F32),
        in_specs=[VMEM_SPEC] * len(args),
        out_specs=VMEM_SPEC,
        scratch_shapes=[pltpu.VMEM((2, TAPS) + got[2].shape, BF16)],
        compiler_params=pltpu.CompilerParams(vmem_limit_bytes=GRANT),
        cost_estimate=pl.CostEstimate(
            flops=4 * cells * rows * chans, bytes_accessed=4 * rows * chans * 4, transcendentals=0
        ),
    )(*args)


def finish_kernel(early_ref, mid_ref, end_ref, kept_ref, w_ref, whole_ref, zpad, sems):
    late, _, _ = places()
    _, hgt, _, chans = end_ref.shape[1:]
    firsts = [pl.ds(*chunk) for chunk in CHUNKS]

    @pl.when(jnp.logical_not(late))
    def _():
        one = fetched(early_ref, whole_ref.at[0, :, firsts[0]], sems.at[0])
        two = fetched(mid_ref, whole_ref.at[0, :, firsts[1]], sems.at[1])
        one.wait()
        two.wait()

    @pl.when(late)
    def _():
        one = fetched(mid_ref, whole_ref.at[0, :, firsts[0]], sems.at[0])
        two = fetched(end_ref.at[:3], whole_ref.at[0, :3, firsts[1]], sems.at[1])
        clear_edges(zpad)
        put_field(zpad, kept_ref[...])
        dx_two = end_ref[3].reshape(-1, chans).astype(F32) + conv_back(zpad, w_ref[0])
        put_field(zpad, dx_two.astype(BF16))
        three = fetched(zpad.at[:, pl.ds(1, hgt)], whole_ref.at[0, 3, firsts[1]], sems.at[2])
        one.wait()
        two.wait()
        three.wait()


def finish(early, mid, end, kept, weights, frames):
    hgt, wid, chans = end.shape[2:]
    args = [early, mid, end, kept, weights]
    return pl.pallas_call(
        finish_kernel,
        out_shape=jax.ShapeDtypeStruct((1, 4, frames, hgt, wid, chans), BF16),
        in_specs=[VMEM_SPEC] * len(args),
        out_specs=HBM_SPEC,
        scratch_shapes=[
            pads(end.shape[1], hgt + 2, wid, chans),
            pltpu.SemaphoreType.DMA((3,)),
        ],
        compiler_params=pltpu.CompilerParams(vmem_limit_bytes=GRANT),
        cost_estimate=pl.CostEstimate(flops=1 << 27, bytes_accessed=1 << 20, transcendentals=0),
        name="finish",
    )(*args)


def momentum_kernel(scale, mom_ref, *refs):
    out_ref = refs[-1]
    total = refs[0][...]
    for ref in refs[1:-1]:
        total = total + ref[...].astype(F32)
    out_ref[0] = 0.9 * mom_ref[0] + total * scale


def shards(incoming, fresh, weights, momentum):
    replicas = lax.axis_size("dp")
    frames = incoming.shape[2]
    per = len(CHUNKS)
    whole = acc = None
    wts = weights
    outs, nears, overs = [], [], []
    for slot in range(TICKS * per + 1):
        near = nears[slot - per] if slot >= per else None
        over = overs[slot - per - 1] if slot > per else None
        got = frame_step(slot, incoming, fresh, wts, acc, whole, near, over)
        outs.append(got[0])
        if slot == 0:
            whole, wts = got[4:]
        if slot <= per * (TICKS - 1):
            near, over = passed_along(got[0], slot)
            nears.append(near)
            overs.append(over)
        if slot < TICKS * per:
            acc = grads_step(got, acc, weights.shape[2])
    kept, *pieces = got[1:]
    terms = [pieces[0]] + [
        lax.ppermute(pieces[k], "dp", [(d, d ^ k) for d in range(replicas)]) for k in ORDER
    ]
    outgoing = finish(*outs[-3:], kept, wts, frames)
    new_momentum = pl.pallas_call(
        functools.partial(momentum_kernel, 1.0 / (TICKS * frames * replicas)),
        out_shape=jax.ShapeDtypeStruct(momentum.shape, F32),
        in_specs=[VMEM_SPEC] * (1 + replicas),
        out_specs=VMEM_SPEC,
        compiler_params=pltpu.CompilerParams(vmem_limit_bytes=GRANT),
        name="momentum",
    )(momentum, *terms)
    return (outgoing, new_momentum)


def solution(mesh):
    return jax.shard_map(
        shards,
        mesh=mesh,
        in_specs=(
            P("segment", None, "dp", None, None, None),
            P(None, None, "dp", None, None, None),
            P("segment", None, None, None),
            P("segment", None, "dp", None),
        ),
        out_specs=(P("segment", None, "dp", None, None, None), P("segment", None, "dp", None)),
        check_vma=False,
    )
```
